32 devices in a mesh: row: 4 (over x, core), col: 8 (over z, y).
Axes of the slice: x: 2, y: 2, z: 4, core: 2. Of those that a mesh axis runs over, the one named last changes fastest.
Arguments:
- matrix: float32 [2048, 2048], P('row', 'col'), as said below
- panel: float32 [2048, 256], P(('row', 'col')), may hold values from -0.125 to 0.125
- factor: float32 [256, 256], replicated, as said below
Outputs:
- updated: float32 [2048, 2048], P('row', 'col')
- correction: float32 [2048, 256], P(('row', 'col'))
The draws below stay inside these ranges and needn't reach their ends.
Inputs may be any that keep to these rules, and one draw needn't show every extreme that they name: `matrix`: symmetric. `factor`: upper triangular with a positive diagonal.
All inputs are finite; a program needn't handle non-finite values.
Results may differ from the reference program's by a relative error of at most 0.000071.
Values sent between devices are 32-bit elements; how exact they have to be, the bound alone decides.
A program may use at most 64 MiB of HBM per device.

```python
import math
import jax
import jax.numpy as jnp
from jax import lax

B = 256
N = 2048


def draw_matrix(key, part):
    noise = jax.random.normal(key, (N, N), jnp.float32)
    return (noise + noise.T) * 0.70710678


def draw_factor(key, part):
    upper = jax.random.normal(jax.random.fold_in(key, 3), (B, B), jnp.float32) * (0.5 / math.sqrt(B))
    diag_vals = jax.random.uniform(jax.random.fold_in(key, 5), (B,), jnp.float32, 0.6, 1.4)
    return jnp.triu(upper, 1) + jnp.diag(diag_vals)


def level_of(stream_key, dims, shards, smallest, high):
    loudness, own = 1.0, jax.random.fold_in(stream_key, 6)
    for dim, shards_of in shards:
        heights = jnp.exp(jax.random.uniform(jax.random.fold_in(own, dim), (shards_of,), jnp.float32, smallest / len(shards), high / len(shards)))
        loudness = loudness * jnp.repeat(heights, dims[dim] // shards_of).reshape([-1 if axis == dim else 1 for axis in range(len(dims))])
    return loudness


def bell_draw(rng, dims, width, limit, pieces=(), dtype=jnp.bfloat16):
    values = jax.random.normal(rng, dims, jnp.float32) * width
    if len(pieces) > 0:
        values = level_of(rng, dims, pieces, -0.22, 0.18) * values
    return jnp.clip(values, min=-limit, max=limit).astype(dtype)


def setup_inputs(seed: int = 0) -> dict:
    keys = jax.random.split(jax.random.key(seed), 4)
    return {
        "matrix": draw_matrix(jax.random.fold_in(keys[3], 71), 0),
        "panel": bell_draw(keys[1], (N, B), N ** -0.5, 0.125, ((0, 32),), jnp.float32),
        "factor": draw_factor(jax.random.fold_in(keys[3], 71), 0),
    }


def mult(left, right):
    return jnp.dot(left, right, precision=lax.Precision.HIGHEST, preferred_element_type=jnp.float32)


def reference(matrix, panel, factor):
    product = mult(matrix, panel)
    scaled = mult(product, factor)
    small = mult(panel.T, scaled)
    correction = scaled - 0.5 * mult(panel, mult(factor.T, small))
    updated = matrix - mult(panel, correction.T) - mult(correction, panel.T)
    return updated, correction
```

```python
import functools

import jax
import jax.numpy as jnp
from jax import lax
from jax.experimental import pallas as pl
from jax.experimental.pallas import tpu as pltpu
from jax.sharding import PartitionSpec as P

F32 = jnp.float32
BF16 = jnp.bfloat16
NN = (((1,), (0,)), ((), ()))
NT = (((1,), (1,)), ((), ()))


def split(x):
    high = x.astype(BF16)
    return high, (x - high.astype(F32)).astype(BF16)


def mult(a, b, dims=NN):
    dot = functools.partial(lax.dot_general, dimension_numbers=dims, preferred_element_type=F32)
    return dot(a[0], b[1]) + dot(a[1], b[0]) + dot(a[0], b[0])


def tile_loop(count, body):
    if count <= 2:
        for i in range(count):
            body(i)
    else:
        pl.loop(0, count)(body)


def kernel(nrows, ncols, tile, a_ref, panel_ref, t_ref, out_ref, corr_ref,
           vr, vc, sr, sc, q, qin, kpart, kin, kfull, at_hi, at_lo, vt_hi, vt_lo,
           v_send, v_recv, vf_send, vf_recv, q_send, q_recv, sc_send, sc_recv,
           s_send, s_recv, sf_send, sf_recv, vc_send, vc_recv, k_send, k_recv, kg_send, kg_recv):
    r, c = lax.axis_index("row"), lax.axis_index("col")
    lines = ncols // 2
    group = ncols // (2 * nrows)
    z, y = c // 2, c % 2
    blk, width = panel_ref.shape
    total = a_ref.shape[0]
    tiles = total // tile
    kblk = width // nrows
    ndev = nrows * ncols
    me = r * ncols + c

    def rows(index, size):
        return pl.ds(pl.multiple_of(index * size, size), size)

    def copy(src, dst, send, recv, row, col):
        return pltpu.make_async_remote_copy(
            src_ref=src, dst_ref=dst, send_sem=send, recv_sem=recv,
            device_id=(row, col), device_id_type=pl.DeviceIdType.MESH)

    barrier = pltpu.get_barrier_semaphore()

    @pl.loop(1, ndev)
    def _(d):
        other = lax.rem(me + d, ndev)
        pl.semaphore_signal(barrier, inc=1, device_id=(other // ncols, lax.rem(other, ncols)),
                            device_id_type=pl.DeviceIdType.MESH)

    vr[rows(c, blk), :] = panel_ref[...]
    pl.semaphore_wait(barrier, ndev - 1)
    sends = []

    def go(desc):
        desc.start()
        sends.append(desc)

    for d in range(1, lines):
        go(copy(panel_ref, vr.at[rows(c, blk)], v_send.at[d], v_recv.at[d], r, lax.rem(z + d, lines) * 2 + y))
    go(copy(panel_ref, vr.at[rows(c, blk)], v_send.at[0], v_recv.at[0], r, z * 2 + 1 - y))

    def flip(i):
        lo_i = pl.ds(pl.multiple_of(i * tile, tile), tile)
        high, low = split(a_ref[lo_i, :].T)
        at_hi[i] = high
        at_lo[i] = low
    tile_loop(tiles, flip)
    t_two = split(t_ref[...])

    for d in range(1, lines):
        source = lax.rem(z - d + lines, lines) * 2 + y
        slot = vr.at[rows(source, blk)]
        copy(panel_ref, slot, v_send.at[d], v_recv.at[d], r, c).wait_recv()
        go(copy(slot, slot, vf_send.at[d], vf_recv.at[d], r, z * 2 + 1 - y))
    copy(panel_ref, vr.at[rows(z * 2 + 1 - y, blk)], v_send.at[0], v_recv.at[0], r, c).wait_recv()
    for d in range(1, lines):
        source = lax.rem(z - d + lines, lines) * 2 + 1 - y
        slot = vr.at[rows(source, blk)]
        copy(slot, slot, vf_send.at[d], vf_recv.at[d], r, c).wait_recv()

    q[...] = jnp.zeros_like(q)

    def gather_product(i):
        q[...] += mult((at_hi[i], at_lo[i]), split(vr[pl.ds(pl.multiple_of(i * tile, tile), tile), :]))
    tile_loop(tiles, gather_product)

    for d in range(1, nrows):
        other = lax.rem(r + d, nrows)
        go(copy(q.at[rows(other, blk)], qin.at[d], q_send.at[d], q_recv.at[d], other, c))

    def turn(i):
        high, low = split(mult(split(vr[pl.ds(pl.multiple_of(i * tile, tile), tile), :]), t_two).T)
        vt_hi[i] = high
        vt_lo[i] = low
    tile_loop(tiles, turn)

    for d in range(1, nrows):
        copy(qin.at[d], qin.at[d], q_send.at[d], q_recv.at[d], r, c).wait_recv()
    product = q[rows(r, blk), :]
    for d in range(1, nrows):
        product = product + qin[d]
    mine = sc.at[rows(r, blk)]
    sc[rows(r, blk), :] = mult(split(product), t_two)

    for d in range(1, nrows):
        go(copy(mine, mine, sc_send.at[d], sc_recv.at[d], lax.rem(r + d, nrows), c))
    target = z // group
    local = lax.rem(c * nrows + r, ncols)
    here = r * group + lax.rem(z, group)
    for d in range(1, lines):
        go(copy(mine, sr.at[rows(local, blk)], s_send.at[d], s_recv.at[here], target,
                lax.rem(z + d, lines) * 2 + y))

    holder = c * nrows // ncols
    v_slice = vr.at[rows(lax.rem(c * nrows, ncols) // nrows, nrows * blk)]

    @pl.when(r == holder)
    def _():
        for d in range(1, nrows):
            copy(v_slice, vc, vc_send.at[d], vc_recv.at[0], lax.rem(r + d, nrows), c).start()
        vc[...] = v_slice[...]

    for d in range(1, nrows):
        slot = sc.at[rows(lax.rem(r - d + nrows, nrows), blk)]
        copy(slot, slot, sc_send.at[d], sc_recv.at[d], r, c).wait_recv()

    for g in range(group):
        line = r * group + g
        for j in range(nrows):
            place = lax.rem((line * 2 + y) * nrows + j, ncols)
            slot = sr.at[rows(place, blk)]

            @pl.when(z == line)
            def _():
                slot[...] = sc[j * blk:(j + 1) * blk, :]

            @pl.when(z != line)
            def _():
                copy(slot, slot, s_send.at[1], s_recv.at[j * group + g], r, c).wait_recv()

            go(copy(slot, slot, sf_send.at[j * group + g], sf_recv.at[j * group + g], r, z * 2 + 1 - y))
    for g in range(group):
        line = r * group + g
        for j in range(nrows):
            place = lax.rem((line * 2 + 1 - y) * nrows + j, ncols)
            slot = sr.at[rows(place, blk)]
            copy(slot, slot, sf_send.at[j * group + g], sf_recv.at[j * group + g], r, c).wait_recv()

    kpart[...] = jnp.zeros_like(kpart)

    def inner(i):
        kpart[...] += mult((vt_hi[i], vt_lo[i]), split(sr[pl.ds(pl.multiple_of(i * tile, tile), tile), :]))
    tile_loop(tiles, inner)

    for d in range(1, nrows):
        other = lax.rem(r + d, nrows)
        go(copy(kpart.at[rows(other, kblk)], kin.at[d], k_send.at[d], k_recv.at[d], other, c))

    @pl.when(r != holder)
    def _():
        copy(vc, vc, vc_send.at[1], vc_recv.at[0], r, c).wait_recv()

    for d in range(1, nrows):
        copy(kin.at[d], kin.at[d], k_send.at[d], k_recv.at[d], r, c).wait_recv()
    summed = kpart[rows(r, kblk), :]
    for d in range(1, nrows):
        summed = summed + kin[d]
    kmine = kfull.at[rows(r, kblk)]
    kfull[rows(r, kblk), :] = summed
    for d in range(1, nrows):
        go(copy(kmine, kmine, kg_send.at[d], kg_recv.at[d], lax.rem(r + d, nrows), c))

    vc_two = split(vc[...])

    def first(i):
        span = pl.ds(pl.multiple_of(i * tile, tile), tile)
        out_ref[span, :] = a_ref[span, :] - mult(split(sr[span, :]), vc_two, NT)
    tile_loop(tiles, first)

    for d in range(1, nrows):
        slot = kfull.at[rows(lax.rem(r - d + nrows, nrows), kblk)]
        copy(slot, slot, kg_send.at[d], kg_recv.at[d], r, c).wait_recv()

    k_two = split(kfull[...])
    y_two = split(sc[...] - mult(vc_two, k_two))

    def second(i):
        span = pl.ds(pl.multiple_of(i * tile, tile), tile)
        out_ref[span, :] = out_ref[span, :] - mult(split(vr[span, :]), y_two, NT)
    tile_loop(tiles, second)
    corr_ref[...] = sr[rows(c, blk), :] - 0.5 * mult(split(panel_ref[...]), k_two)

    for desc in sends:
        desc.wait_send()

    @pl.when(r == holder)
    def _():
        for d in range(1, nrows):
            copy(v_slice, vc, vc_send.at[d], vc_recv.at[0], r, c).wait_send()


def per_device(nrows, ncols, matrix, panel, factor):
    total, wide = matrix.shape
    blk, width = panel.shape
    tile = min(256, total)
    tiles = total // tile
    group = ncols // (2 * nrows)
    lines = ncols // 2
    dma = pltpu.SemaphoreType.DMA
    vmem = pl.BlockSpec(memory_space=pltpu.VMEM)
    return pl.pallas_call(
        functools.partial(kernel, nrows, ncols, tile),
        out_shape=(jax.ShapeDtypeStruct(matrix.shape, F32), jax.ShapeDtypeStruct(panel.shape, F32)),
        in_specs=[vmem] * 3,
        out_specs=(vmem, vmem),
        scratch_shapes=[
            pltpu.VMEM((total, width), F32),
            pltpu.VMEM((wide, width), F32),
            pltpu.VMEM((total, width), F32),
            pltpu.VMEM((wide, width), F32),
            pltpu.VMEM((wide, width), F32),
            pltpu.VMEM((nrows, blk, width), F32),
            pltpu.VMEM((width, width), F32),
            pltpu.VMEM((nrows, width // nrows, width), F32),
            pltpu.VMEM((width, width), F32),
            pltpu.VMEM((tiles, wide, tile), BF16),
            pltpu.VMEM((tiles, wide, tile), BF16),
            pltpu.VMEM((tiles, width, tile), BF16),
            pltpu.VMEM((tiles, width, tile), BF16),
            dma((lines,)), dma((lines,)), dma((lines,)), dma((lines,)),
            dma((nrows,)), dma((nrows,)), dma((nrows,)), dma((nrows,)),
            dma((lines,)), dma((nrows * group,)), dma((nrows * group,)), dma((nrows * group,)),
            dma((nrows,)), dma((1,)), dma((nrows,)), dma((nrows,)), dma((nrows,)), dma((nrows,)),
        ],
        compiler_params=pltpu.CompilerParams(
            collective_id=0, has_side_effects=True, vmem_limit_bytes=60 * 1024 * 1024),
    )(matrix, panel, factor)


def solution(mesh):
    in_specs = (P("row", "col"), P(("row", "col"), None), P())
    out_specs = (P("row", "col"), P(("row", "col"), None))
    return jax.shard_map(
        functools.partial(per_device, mesh.shape["row"], mesh.shape["col"]),
        mesh=mesh, in_specs=in_specs, out_specs=out_specs, check_vma=False)
```

```python
import functools

import jax
import jax.numpy as jnp
from jax import lax
from jax.experimental import pallas as pl
from jax.experimental.pallas import tpu as pltpu
from jax.sharding import PartitionSpec as P

F32 = jnp.float32
BF16 = jnp.bfloat16
NN = (((1,), (0,)), ((), ()))
NT = (((1,), (1,)), ((), ()))


def split(x):
    high = x.astype(BF16)
    return high, (x - high.astype(F32)).astype(BF16)


def mult(a, b, dims=NN):
    dot = functools.partial(lax.dot_general, dimension_numbers=dims, preferred_element_type=F32)
    return dot(a[0], b[1]) + dot(a[1], b[0]) + dot(a[0], b[0])


def tile_loop(count, body):
    if count <= 2:
        for i in range(count):
            body(i)
    else:
        pl.loop(0, count)(body)


def kernel(nrows, ncols, tile, a_ref, panel_ref, t_ref, out_ref, corr_ref,
           vr, vc, sr, sc, q, qin, kpart, kin, kpair, kfull, at_hi, at_lo, vt_hi, vt_lo,
           v_send, v_recv, vf_send, vf_recv, q_send, q_recv, sc_send, sc_recv,
           s_send, s_recv, sf_send, sf_recv, vc_send, vc_recv, k_send, k_recv, kg_send, kg_recv):
    r, c = lax.axis_index("row"), lax.axis_index("col")
    lines = ncols // 2
    group = ncols // (2 * nrows)
    z, y = c // 2, c % 2
    blk, width = panel_ref.shape
    total = a_ref.shape[0]
    tiles = total // tile
    half = width // 2
    mate = r + 1 - 2 * (r % 2)

    def rows(index, size):
        return pl.ds(pl.multiple_of(index * size, size), size)

    def copy(src, dst, send, recv, row, col):
        return pltpu.make_async_remote_copy(
            src_ref=src, dst_ref=dst, send_sem=send, recv_sem=recv,
            device_id=(row, col), device_id_type=pl.DeviceIdType.MESH)

    barrier = pltpu.get_barrier_semaphore()

    def greet(row, col):
        pl.semaphore_signal(barrier, inc=1, device_id=(row, col), device_id_type=pl.DeviceIdType.MESH)

    target = z // group
    for d in range(1, lines):
        greet(r, lax.rem(z + d, lines) * 2 + y)
    greet(r, z * 2 + 1 - y)
    for d in range(1, nrows):
        greet(lax.rem(r + d, nrows), c)
    for g in range(group):
        line = r * group + g

        @pl.when(z != line)
        def _():
            for d in range(1, nrows):
                greet(lax.rem(r + d, nrows), line * 2 + y)

    vr[rows(c, blk), :] = panel_ref[...]
    pl.semaphore_wait(barrier, lines + nrows - 1 + jnp.where(target == r, 0, lines - 1))
    sends = []
    vc_sent = []

    def finish():
        for desc in sends:
            desc.wait_send()
        if vc_sent:
            @pl.when(r == holder)
            def _():
                for d in range(1, nrows):
                    copy(v_slice, vc, vc_send.at[d], vc_recv.at[0], lax.rem(r + d, nrows), c).wait_send()

    def go(desc):
        desc.start()
        sends.append(desc)

    for d in range(1, lines):
        go(copy(panel_ref, vr.at[rows(c, blk)], v_send.at[d], v_recv.at[d], r, lax.rem(z + d, lines) * 2 + y))
    go(copy(panel_ref, vr.at[rows(c, blk)], v_send.at[0], v_recv.at[0], r, z * 2 + 1 - y))

    def flip(i):
        lo_i = pl.ds(pl.multiple_of(i * tile, tile), tile)
        high, low = split(a_ref[lo_i, :].T)
        at_hi[i] = high
        at_lo[i] = low
    tile_loop(tiles, flip)
    t_two = split(t_ref[...])

    for d in range(1, lines):
        source = lax.rem(z - d + lines, lines) * 2 + y
        slot = vr.at[rows(source, blk)]
        copy(panel_ref, slot, v_send.at[d], v_recv.at[d], r, c).wait_recv()
        go(copy(slot, slot, vf_send.at[d], vf_recv.at[d], r, z * 2 + 1 - y))
    copy(panel_ref, vr.at[rows(z * 2 + 1 - y, blk)], v_send.at[0], v_recv.at[0], r, c).wait_recv()
    for d in range(1, lines):
        source = lax.rem(z - d + lines, lines) * 2 + 1 - y
        slot = vr.at[rows(source, blk)]
        copy(slot, slot, vf_send.at[d], vf_recv.at[d], r, c).wait_recv()

    q[...] = jnp.zeros_like(q)

    def gather_product(i):
        q[...] += mult((at_hi[i], at_lo[i]), split(vr[pl.ds(pl.multiple_of(i * tile, tile), tile), :]))
    tile_loop(tiles, gather_product)

    for d in range(1, nrows):
        other = lax.rem(r + d, nrows)
        go(copy(q.at[rows(other, blk)], qin.at[d], q_send.at[d], q_recv.at[d], other, c))

    def turn(i):
        high, low = split(mult(split(vr[pl.ds(pl.multiple_of(i * tile, tile), tile), :]), t_two).T)
        vt_hi[i] = high
        vt_lo[i] = low
    tile_loop(tiles, turn)

    for d in range(1, nrows):
        copy(qin.at[d], qin.at[d], q_send.at[d], q_recv.at[d], r, c).wait_recv()
    product = q[rows(r, blk), :]
    for d in range(1, nrows):
        product = product + qin[d]
    mine = sc.at[rows(r, blk)]
    sc[rows(r, blk), :] = mult(split(product), t_two)

    for d in range(1, nrows):
        go(copy(mine, mine, sc_send.at[d], sc_recv.at[d], lax.rem(r + d, nrows), c))
    local = lax.rem(c * nrows + r, ncols)
    here = r * group + lax.rem(z, group)
    for d in range(1, lines):
        go(copy(mine, sr.at[rows(local, blk)], s_send.at[d], s_recv.at[here], target,
                lax.rem(z + d, lines) * 2 + y))

    holder = c * nrows // ncols
    v_slice = vr.at[rows(lax.rem(c * nrows, ncols) // nrows, nrows * blk)]

    vc_sent.append(True)

    @pl.when(r == holder)
    def _():
        for d in range(1, nrows):
            copy(v_slice, vc, vc_send.at[d], vc_recv.at[0], lax.rem(r + d, nrows), c).start()
        vc[...] = v_slice[...]

    for d in range(1, nrows):
        slot = sc.at[rows(lax.rem(r - d + nrows, nrows), blk)]
        copy(slot, slot, sc_send.at[d], sc_recv.at[d], r, c).wait_recv()

    for g in range(group):
        line = r * group + g
        for j in range(nrows):
            place = lax.rem((line * 2 + y) * nrows + j, ncols)
            slot = sr.at[rows(place, blk)]

            @pl.when(z == line)
            def _():
                slot[...] = sc[j * blk:(j + 1) * blk, :]

            @pl.when(z != line)
            def _():
                copy(slot, slot, s_send.at[1], s_recv.at[j * group + g], r, c).wait_recv()

            go(copy(slot, slot, sf_send.at[j * group + g], sf_recv.at[j * group + g], r, z * 2 + 1 - y))
    for g in range(group):
        line = r * group + g
        for j in range(nrows):
            place = lax.rem((line * 2 + 1 - y) * nrows + j, ncols)
            slot = sr.at[rows(place, blk)]
            copy(slot, slot, sf_send.at[j * group + g], sf_recv.at[j * group + g], r, c).wait_recv()

    kpart[...] = jnp.zeros_like(kpart)

    def inner(i):
        kpart[...] += mult((vt_hi[i], vt_lo[i]), split(sr[pl.ds(pl.multiple_of(i * tile, tile), tile), :]))
    tile_loop(tiles, inner)

    go(copy(kpart.at[rows(mate % 2, half)], kin.at[0], k_send.at[0], k_recv.at[0], mate, c))

    @pl.when(r != holder)
    def _():
        copy(vc, vc, vc_send.at[1], vc_recv.at[0], r, c).wait_recv()

    copy(kin.at[0], kin.at[0], k_send.at[0], k_recv.at[0], r, c).wait_recv()
    kpair[...] = kpart[rows(r % 2, half), :] + kin[0]
    for d in range(1, nrows // 2):
        go(copy(kpair, kin.at[d], k_send.at[d], k_recv.at[d], lax.rem(r + 2 * d, nrows), c))

    vc_two = split(vc[...])

    def first(i):
        span = pl.ds(pl.multiple_of(i * tile, tile), tile)
        out_ref[span, :] = a_ref[span, :] - mult(split(sr[span, :]), vc_two, NT)
    tile_loop(tiles, first)

    for d in range(1, nrows // 2):
        copy(kpair, kin.at[d], k_send.at[d], k_recv.at[d], r, c).wait_recv()
    summed = kpair[...]
    for d in range(1, nrows // 2):
        summed = summed + kin[d]
    mine_half = kfull.at[rows(r % 2, half)]
    mine_half[...] = summed
    go(copy(mine_half, mine_half, kg_send.at[0], kg_recv.at[0], mate, c))
    other_half = kfull.at[rows(mate % 2, half)]
    copy(other_half, other_half, kg_send.at[0], kg_recv.at[0], r, c).wait_recv()

    k_two = split(kfull[...])
    y_two = split(sc[...] - mult(vc_two, k_two))

    def second(i):
        span = pl.ds(pl.multiple_of(i * tile, tile), tile)
        out_ref[span, :] = out_ref[span, :] - mult(split(vr[span, :]), y_two, NT)
    tile_loop(tiles, second)
    corr_ref[...] = sr[rows(c, blk), :] - 0.5 * mult(split(panel_ref[...]), k_two)

    finish()


def per_device(nrows, ncols, matrix, panel, factor):
    total, wide = matrix.shape
    blk, width = panel.shape
    tile = min(256, total)
    tiles = total // tile
    group = ncols // (2 * nrows)
    lines = ncols // 2
    dma = pltpu.SemaphoreType.DMA
    vmem = pl.BlockSpec(memory_space=pltpu.VMEM)
    return pl.pallas_call(
        functools.partial(kernel, nrows, ncols, tile),
        out_shape=(jax.ShapeDtypeStruct(matrix.shape, F32), jax.ShapeDtypeStruct(panel.shape, F32)),
        in_specs=[vmem] * 3,
        out_specs=(vmem, vmem),
        scratch_shapes=[
            pltpu.VMEM((total, width), F32),
            pltpu.VMEM((wide, width), F32),
            pltpu.VMEM((total, width), F32),
            pltpu.VMEM((wide, width), F32),
            pltpu.VMEM((wide, width), F32),
            pltpu.VMEM((nrows, blk, width), F32),
            pltpu.VMEM((width, width), F32),
            pltpu.VMEM((nrows // 2, width // 2, width), F32),
            pltpu.VMEM((width // 2, width), F32),
            pltpu.VMEM((width, width), F32),
            pltpu.VMEM((tiles, wide, tile), BF16),
            pltpu.VMEM((tiles, wide, tile), BF16),
            pltpu.VMEM((tiles, width, tile), BF16),
            pltpu.VMEM((tiles, width, tile), BF16),
            dma((lines,)), dma((lines,)), dma((lines,)), dma((lines,)),
            dma((nrows,)), dma((nrows,)), dma((nrows,)), dma((nrows,)),
            dma((lines,)), dma((nrows * group,)), dma((nrows * group,)), dma((nrows * group,)),
            dma((nrows,)), dma((1,)), dma((nrows,)), dma((nrows,)), dma((nrows,)), dma((nrows,)),
        ],
        compiler_params=pltpu.CompilerParams(
            collective_id=0, has_side_effects=True, vmem_limit_bytes=60 * 1024 * 1024),
    )(matrix, panel, factor)


def solution(mesh):
    in_specs = (P("row", "col"), P(("row", "col"), None), P())
    out_specs = (P("row", "col"), P(("row", "col"), None))
    return jax.shard_map(
        functools.partial(per_device, mesh.shape["row"], mesh.shape["col"]),
        mesh=mesh, in_specs=in_specs, out_specs=out_specs, check_vma=False)
```

```python
import functools

import jax
import jax.numpy as jnp
from jax import lax
from jax.experimental import pallas as pl
from jax.experimental.pallas import tpu as pltpu
from jax.sharding import PartitionSpec as P

F32 = jnp.float32
BF16 = jnp.bfloat16
NN = (((1,), (0,)), ((), ()))
NT = (((1,), (1,)), ((), ()))


def split(x):
    high = x.astype(BF16)
    return high, (x - high.astype(F32)).astype(BF16)


def mult(a, b, dims=NN):
    dot = functools.partial(lax.dot_general, dimension_numbers=dims, preferred_element_type=F32)
    return dot(a[0], b[1]) + dot(a[1], b[0]) + dot(a[0], b[0])


def tile_loop(count, body):
    if count <= 2:
        for i in range(count):
            body(i)
    else:
        pl.loop(0, count)(body)


def kernel(nrows, ncols, tile, a_ref, panel_ref, t_ref, out_ref, corr_ref,
           vr, vc, sr, sc, q, qin, kpart, kin, kpair, kfull, at_hi, at_lo, vt_hi, vt_lo,
           v_send, v_recv, vf_send, vf_recv, q_send, q_recv, sc_send, sc_recv,
           s_send, s_recv, sf_send, sf_recv, vc_send, vc_recv, k_send, k_recv, kg_send, kg_recv):
    r, c = lax.axis_index("row"), lax.axis_index("col")
    lines = ncols // 2
    group = ncols // (2 * nrows)
    z, y = c // 2, c % 2
    blk, width = panel_ref.shape
    total = a_ref.shape[0]
    tiles = total // tile
    half = width // 2
    mate = r + 1 - 2 * (r % 2)

    def rows(index, size):
        return pl.ds(pl.multiple_of(index * size, size), size)

    def copy(src, dst, send, recv, row, col):
        return pltpu.make_async_remote_copy(
            src_ref=src, dst_ref=dst, send_sem=send, recv_sem=recv,
            device_id=(row, col), device_id_type=pl.DeviceIdType.MESH)

    barrier = pltpu.get_barrier_semaphore()

    def greet(row, col):
        pl.semaphore_signal(barrier, inc=1, device_id=(row, col), device_id_type=pl.DeviceIdType.MESH)

    target = z // group
    for d in range(1, lines):
        greet(r, lax.rem(z + d, lines) * 2 + y)
    greet(r, z * 2 + 1 - y)
    for d in range(1, nrows):
        greet(lax.rem(r + d, nrows), c)
    for g in range(group):
        line = r * group + g

        @pl.when(z != line)
        def _():
            for d in range(1, nrows):
                greet(lax.rem(r + d, nrows), line * 2 + y)

    vr[rows(c, blk), :] = panel_ref[...]
    pl.semaphore_wait(barrier, lines + nrows - 1 + jnp.where(target == r, 0, lines - 1))
    sends = []
    holder = c * nrows // ncols
    first_block = lax.rem(c * nrows, ncols)
    near = sorted((o for o in range(1 - lines, lines) if o), key=abs)

    def each_line(offsets, body):
        for o in offsets:
            line = z + o
            pl.when((line >= 0) & (line < lines))(functools.partial(body, line))

    def finish():
        for desc in sends:
            desc.wait_send()
        for d in range(lines):
            line = lax.rem(z + d, lines)
            copy(panel_ref, panel_ref, v_send.at[line], v_recv.at[line], r, c).wait_send()
            if d:
                copy(panel_ref, panel_ref, vf_send.at[line], vf_recv.at[line], r, c).wait_send()
                copy(panel_ref, panel_ref, s_send.at[line], s_recv.at[0], r, c).wait_send()

        for i in range(nrows * group):
            copy(panel_ref, panel_ref, sf_send.at[i], sf_recv.at[i], r, c).wait_send()

        @pl.when(r == holder)
        def _():
            for d in range(1, nrows):
                for j in range(nrows):
                    copy(panel_ref, panel_ref, vc_send.at[d, j], vc_recv.at[j], r, c).wait_send()

    def go(desc):
        desc.start()
        sends.append(desc)

    def pass_on(src, column):
        j = column - first_block

        @pl.when((r == holder) & (j >= 0) & (j < nrows))
        def _():
            for d in range(1, nrows):
                copy(src, vc.at[rows(j, blk)], vc_send.at[d, j], vc_recv.at[j],
                     lax.rem(r + d, nrows), c).start()

    across = z * 2 + 1 - y
    own = vr.at[rows(c, blk)]
    copy(panel_ref, own, v_send.at[z], v_recv.at[z], r, across).start()

    def send_panel(line):
        copy(panel_ref, own, v_send.at[line], v_recv.at[z], r, line * 2 + y).start()
    each_line(near, send_panel)
    pass_on(panel_ref, c)

    def flip(i):
        lo_i = pl.ds(pl.multiple_of(i * tile, tile), tile)
        high, low = split(a_ref[lo_i, :].T)
        at_hi[i] = high
        at_lo[i] = low
    tile_loop(tiles, flip)
    t_two = split(t_ref[...])

    def forward(line):
        slot = vr.at[rows(line * 2 + y, blk)]
        copy(slot, slot, v_send.at[line], v_recv.at[line], r, c).wait_recv()
        copy(slot, slot, vf_send.at[line], vf_recv.at[line], r, across).start()
        pass_on(slot, line * 2 + y)

    def arrive(line):
        slot = vr.at[rows(line * 2 + 1 - y, blk)]
        copy(slot, slot, vf_send.at[line], vf_recv.at[line], r, c).wait_recv()
        pass_on(slot, line * 2 + 1 - y)

    each_line(near[:2], forward)
    slot = vr.at[rows(across, blk)]
    copy(slot, slot, v_send.at[z], v_recv.at[z], r, c).wait_recv()
    pass_on(slot, across)
    each_line(near[2:], forward)
    each_line(near, arrive)

    q[...] = jnp.zeros_like(q)

    def gather_product(i):
        q[...] += mult((at_hi[i], at_lo[i]), split(vr[pl.ds(pl.multiple_of(i * tile, tile), tile), :]))
    tile_loop(tiles, gather_product)

    for d in range(1, nrows):
        other = lax.rem(r + d, nrows)
        go(copy(q.at[rows(other, blk)], qin.at[d], q_send.at[d], q_recv.at[d], other, c))

    def turn(i):
        high, low = split(mult(split(vr[pl.ds(pl.multiple_of(i * tile, tile), tile), :]), t_two).T)
        vt_hi[i] = high
        vt_lo[i] = low
    tile_loop(tiles, turn)

    for d in range(1, nrows):
        copy(qin.at[d], qin.at[d], q_send.at[d], q_recv.at[d], r, c).wait_recv()
    product = q[rows(r, blk), :]
    for d in range(1, nrows):
        product = product + qin[d]
    mine = sc.at[rows(r, blk)]
    sc[rows(r, blk), :] = mult(split(product), t_two)

    local = lax.rem(c * nrows + r, ncols)
    here = r * group + lax.rem(z, group)

    def send_scaled(line):
        copy(mine, sr.at[rows(local, blk)], s_send.at[line], s_recv.at[here], target, line * 2 + y).start()
    each_line(near[::-1], send_scaled)
    for d in range(1, nrows):
        go(copy(mine, mine, sc_send.at[d], sc_recv.at[d], lax.rem(r + d, nrows), c))

    @pl.when(r == holder)
    def _():
        vc[...] = vr[rows(first_block // nrows, nrows * blk), :]

    for d in range(1, nrows):
        slot = sc.at[rows(lax.rem(r - d + nrows, nrows), blk)]
        copy(slot, slot, sc_send.at[d], sc_recv.at[d], r, c).wait_recv()

    for g in range(group):
        line = r * group + g
        for d in range(nrows):
            j = lax.rem(r + d, nrows)
            place = lax.rem((line * 2 + y) * nrows + j, ncols)
            slot = sr.at[rows(place, blk)]

            @pl.when(z == line)
            def _():
                held = sc.at[rows(j, blk)]
                copy(held, slot, sf_send.at[j * group + g], sf_recv.at[j * group + g], r, across).start()
                slot[...] = held[...]

            @pl.when(z != line)
            def _():
                copy(slot, slot, s_send.at[0], s_recv.at[j * group + g], r, c).wait_recv()
                copy(slot, slot, sf_send.at[j * group + g], sf_recv.at[j * group + g], r, across).start()
    for g in range(group):
        line = r * group + g
        for j in range(nrows):
            place = lax.rem((line * 2 + 1 - y) * nrows + j, ncols)
            slot = sr.at[rows(place, blk)]
            copy(slot, slot, sf_send.at[j * group + g], sf_recv.at[j * group + g], r, c).wait_recv()

    kpart[...] = jnp.zeros_like(kpart)

    def inner(i):
        kpart[...] += mult((vt_hi[i], vt_lo[i]), split(sr[pl.ds(pl.multiple_of(i * tile, tile), tile), :]))
    tile_loop(tiles, inner)

    go(copy(kpart.at[rows(mate % 2, half)], kin.at[0], k_send.at[0], k_recv.at[0], mate, c))

    @pl.when(r != holder)
    def _():
        for j in range(nrows):
            copy(panel_ref, panel_ref, vc_send.at[1, j], vc_recv.at[j], r, c).wait_recv()

    copy(kin.at[0], kin.at[0], k_send.at[0], k_recv.at[0], r, c).wait_recv()
    kpair[...] = kpart[rows(r % 2, half), :] + kin[0]
    for d in range(1, nrows // 2):
        go(copy(kpair, kin.at[d], k_send.at[d], k_recv.at[d], lax.rem(r + 2 * d, nrows), c))

    vc_two = split(vc[...])

    def first(i):
        span = pl.ds(pl.multiple_of(i * tile, tile), tile)
        out_ref[span, :] = a_ref[span, :] - mult(split(sr[span, :]), vc_two, NT)
    tile_loop(tiles, first)

    for d in range(1, nrows // 2):
        copy(kpair, kin.at[d], k_send.at[d], k_recv.at[d], r, c).wait_recv()
    summed = kpair[...]
    for d in range(1, nrows // 2):
        summed = summed + kin[d]
    mine_half = kfull.at[rows(r % 2, half)]
    mine_half[...] = summed
    go(copy(mine_half, mine_half, kg_send.at[0], kg_recv.at[0], mate, c))
    other_half = kfull.at[rows(mate % 2, half)]
    copy(other_half, other_half, kg_send.at[0], kg_recv.at[0], r, c).wait_recv()

    k_two = split(kfull[...])
    y_two = split(sc[...] - mult(vc_two, k_two))

    def second(i):
        span = pl.ds(pl.multiple_of(i * tile, tile), tile)
        out_ref[span, :] = out_ref[span, :] - mult(split(vr[span, :]), y_two, NT)
    tile_loop(tiles, second)
    corr_ref[...] = sr[rows(c, blk), :] - 0.5 * mult(split(panel_ref[...]), k_two)

    finish()


def per_device(nrows, ncols, matrix, panel, factor):
    total, wide = matrix.shape
    blk, width = panel.shape
    tile = min(256, total)
    tiles = total // tile
    group = ncols // (2 * nrows)
    lines = ncols // 2
    dma = pltpu.SemaphoreType.DMA
    vmem = pl.BlockSpec(memory_space=pltpu.VMEM)
    return pl.pallas_call(
        functools.partial(kernel, nrows, ncols, tile),
        out_shape=(jax.ShapeDtypeStruct(matrix.shape, F32), jax.ShapeDtypeStruct(panel.shape, F32)),
        in_specs=[vmem] * 3,
        out_specs=(vmem, vmem),
        scratch_shapes=[
            pltpu.VMEM((total, width), F32),
            pltpu.VMEM((wide, width), F32),
            pltpu.VMEM((total, width), F32),
            pltpu.VMEM((wide, width), F32),
            pltpu.VMEM((wide, width), F32),
            pltpu.VMEM((nrows, blk, width), F32),
            pltpu.VMEM((width, width), F32),
            pltpu.VMEM((nrows // 2, width // 2, width), F32),
            pltpu.VMEM((width // 2, width), F32),
            pltpu.VMEM((width, width), F32),
            pltpu.VMEM((tiles, wide, tile), BF16),
            pltpu.VMEM((tiles, wide, tile), BF16),
            pltpu.VMEM((tiles, width, tile), BF16),
            pltpu.VMEM((tiles, width, tile), BF16),
            dma((lines,)), dma((lines,)), dma((lines,)), dma((lines,)),
            dma((nrows,)), dma((nrows,)), dma((nrows,)), dma((nrows,)),
            dma((lines,)), dma((nrows * group,)), dma((nrows * group,)), dma((nrows * group,)),
            dma((nrows, nrows)), dma((nrows,)), dma((nrows,)), dma((nrows,)), dma((nrows,)), dma((nrows,)),
        ],
        compiler_params=pltpu.CompilerParams(
            collective_id=0, has_side_effects=True, vmem_limit_bytes=60 * 1024 * 1024),
    )(matrix, panel, factor)


def solution(mesh):
    in_specs = (P("row", "col"), P(("row", "col"), None), P())
    out_specs = (P("row", "col"), P(("row", "col"), None))
    return jax.shard_map(
        functools.partial(per_device, mesh.shape["row"], mesh.shape["col"]),
        mesh=mesh, in_specs=in_specs, out_specs=out_specs, check_vma=False)
```

```python
import functools

import jax
import jax.numpy as jnp
from jax import lax
from jax.experimental import pallas as pl
from jax.experimental.pallas import tpu as pltpu
from jax.sharding import PartitionSpec as P

F32 = jnp.float32
BF16 = jnp.bfloat16
NN = (((1,), (0,)), ((), ()))
NT = (((1,), (1,)), ((), ()))


def split(x):
    high = x.astype(BF16)
    return high, (x - high.astype(F32)).astype(BF16)


def mult(a, b, dims=NN):
    dot = functools.partial(lax.dot_general, dimension_numbers=dims, preferred_element_type=F32)
    return dot(a[0], b[1]) + dot(a[1], b[0]) + dot(a[0], b[0])


def tile_loop(count, body):
    if count <= 2:
        for i in range(count):
            body(i)
    else:
        pl.loop(0, count)(body)


def kernel(nrows, ncols, tile, a_ref, panel_ref, t_ref, out_ref, corr_ref,
           vr, vc, sr, sc, q, qin, kpart, kin, kpair, kfull, at_hi, at_lo, vt_hi, vt_lo,
           v_send, v_recv, vf_send, vf_recv, q_send, q_recv, sc_send, sc_recv,
           s_send, s_recv, sf_send, sf_recv, vc_send, vc_recv, k_send, k_recv, kg_send, kg_recv):
    r, c = lax.axis_index("row"), lax.axis_index("col")
    lines = ncols // 2
    group = ncols // (2 * nrows)
    z, y = c // 2, c % 2
    blk, width = panel_ref.shape
    total = a_ref.shape[0]
    tiles = total // tile
    half = width // 2
    mate = r + 1 - 2 * (r % 2)

    def rows(index, size):
        return pl.ds(pl.multiple_of(index * size, size), size)

    def copy(src, dst, send, recv, row, col):
        return pltpu.make_async_remote_copy(
            src_ref=src, dst_ref=dst, send_sem=send, recv_sem=recv,
            device_id=(row, col), device_id_type=pl.DeviceIdType.MESH)

    barrier = pltpu.get_barrier_semaphore()

    def greet(row, col):
        pl.semaphore_signal(barrier, inc=1, device_id=(row, col), device_id_type=pl.DeviceIdType.MESH)

    target = z // group
    for d in range(1, lines):
        greet(r, lax.rem(z + d, lines) * 2 + y)
    greet(r, z * 2 + 1 - y)
    for d in range(1, nrows):
        greet(lax.rem(r + d, nrows), c)
    for g in range(group):
        line = r * group + g

        @pl.when(z != line)
        def _():
            for d in range(1, nrows):
                greet(lax.rem(r + d, nrows), line * 2 + y)

    vr[rows(c, blk), :] = panel_ref[...]
    pl.semaphore_wait(barrier, lines + nrows - 1 + jnp.where(target == r, 0, lines - 1))
    sends = []
    holder = c * nrows // ncols
    first_block = lax.rem(c * nrows, ncols)
    near = sorted((o for o in range(1 - lines, lines) if o), key=abs)

    def each_line(offsets, body):
        for o in offsets:
            line = z + o
            pl.when((line >= 0) & (line < lines))(functools.partial(body, line))

    def finish():
        for desc in sends:
            desc.wait_send()
        for d in range(lines):
            line = lax.rem(z + d, lines)
            copy(panel_ref, panel_ref, v_send.at[line], v_recv.at[line], r, c).wait_send()
            if d:
                copy(panel_ref, panel_ref, vf_send.at[line], vf_recv.at[line], r, c).wait_send()
                copy(panel_ref, panel_ref, s_send.at[line], s_recv.at[0], r, c).wait_send()

        for i in range(nrows * group):
            copy(panel_ref, panel_ref, sf_send.at[i], sf_recv.at[i], r, c).wait_send()

        @pl.when(r % 2 == holder % 2)
        def _():
            copy(vc, vc, vc_send.at[0], vc_recv.at[0], r, c).wait_send()

        @pl.when(r == holder)
        def _():
            for d in range(1, nrows // 2):
                copy(vc, vc, vc_send.at[d], vc_recv.at[0], r, c).wait_send()

    def go(desc):
        desc.start()
        sends.append(desc)

    across = z * 2 + 1 - y
    own = vr.at[rows(c, blk)]
    copy(panel_ref, own, v_send.at[z], v_recv.at[z], r, across).start()

    def send_panel(line):
        copy(panel_ref, own, v_send.at[line], v_recv.at[z], r, line * 2 + y).start()
    each_line(near, send_panel)

    def flip(i):
        lo_i = pl.ds(pl.multiple_of(i * tile, tile), tile)
        high, low = split(a_ref[lo_i, :].T)
        at_hi[i] = high
        at_lo[i] = low
    tile_loop(tiles, flip)
    t_two = split(t_ref[...])

    def forward(line):
        slot = vr.at[rows(line * 2 + y, blk)]
        copy(slot, slot, v_send.at[line], v_recv.at[line], r, c).wait_recv()
        copy(slot, slot, vf_send.at[line], vf_recv.at[line], r, across).start()

    def arrive(line):
        slot = vr.at[rows(line * 2 + 1 - y, blk)]
        copy(slot, slot, vf_send.at[line], vf_recv.at[line], r, c).wait_recv()

    each_line(near[:2], forward)
    slot = vr.at[rows(across, blk)]
    copy(slot, slot, v_send.at[z], v_recv.at[z], r, c).wait_recv()
    each_line(near[2:], forward)
    each_line(near, arrive)

    q[...] = jnp.zeros_like(q)

    def gather_product(i):
        q[...] += mult((at_hi[i], at_lo[i]), split(vr[pl.ds(pl.multiple_of(i * tile, tile), tile), :]))
    tile_loop(tiles, gather_product)

    for d in range(1, nrows):
        other = lax.rem(r + d, nrows)
        go(copy(q.at[rows(other, blk)], qin.at[d], q_send.at[d], q_recv.at[d], other, c))

    def turn(i):
        high, low = split(mult(split(vr[pl.ds(pl.multiple_of(i * tile, tile), tile), :]), t_two).T)
        vt_hi[i] = high
        vt_lo[i] = low
    tile_loop(tiles, turn)

    for d in range(1, nrows):
        copy(qin.at[d], qin.at[d], q_send.at[d], q_recv.at[d], r, c).wait_recv()
    product = q[rows(r, blk), :]
    for d in range(1, nrows):
        product = product + qin[d]
    mine = sc.at[rows(r, blk)]
    sc[rows(r, blk), :] = mult(split(product), t_two)

    local = lax.rem(c * nrows + r, ncols)
    here = r * group + lax.rem(z, group)

    def send_scaled(line):
        copy(mine, sr.at[rows(local, blk)], s_send.at[line], s_recv.at[here], target, line * 2 + y).start()
    each_line(near[::-1], send_scaled)
    for d in range(1, nrows):
        go(copy(mine, mine, sc_send.at[d], sc_recv.at[d], lax.rem(r + d, nrows), c))

    for d in range(1, nrows):
        slot = sc.at[rows(lax.rem(r - d + nrows, nrows), blk)]
        copy(slot, slot, sc_send.at[d], sc_recv.at[d], r, c).wait_recv()

    for g in range(group):
        line = r * group + g
        for d in range(nrows):
            j = lax.rem(r + d, nrows)
            place = lax.rem((line * 2 + y) * nrows + j, ncols)
            slot = sr.at[rows(place, blk)]

            @pl.when(z == line)
            def _():
                held = sc.at[rows(j, blk)]
                copy(held, slot, sf_send.at[j * group + g], sf_recv.at[j * group + g], r, across).start()
                slot[...] = held[...]

            @pl.when(z != line)
            def _():
                copy(slot, slot, s_send.at[0], s_recv.at[j * group + g], r, c).wait_recv()
                copy(slot, slot, sf_send.at[j * group + g], sf_recv.at[j * group + g], r, across).start()
    @pl.when(r == holder)
    def _():
        v_slice = vr.at[rows(first_block // nrows, nrows * blk)]
        for d in range(1, nrows // 2):
            copy(v_slice, vc, vc_send.at[d], vc_recv.at[0], lax.rem(r + 2 * d, nrows), c).start()
        copy(v_slice, vc, vc_send.at[0], vc_recv.at[0], mate, c).start()
        vc[...] = v_slice[...]

    for g in range(group):
        line = r * group + g
        for j in range(nrows):
            place = lax.rem((line * 2 + 1 - y) * nrows + j, ncols)
            slot = sr.at[rows(place, blk)]
            copy(slot, slot, sf_send.at[j * group + g], sf_recv.at[j * group + g], r, c).wait_recv()

    kpart[...] = jnp.zeros_like(kpart)

    def inner(i):
        kpart[...] += mult((vt_hi[i], vt_lo[i]), split(sr[pl.ds(pl.multiple_of(i * tile, tile), tile), :]))
    tile_loop(tiles, inner)

    go(copy(kpart.at[rows(mate % 2, half)], kin.at[0], k_send.at[0], k_recv.at[0], mate, c))

    @pl.when(r != holder)
    def _():
        copy(vc, vc, vc_send.at[0], vc_recv.at[0], r, c).wait_recv()

    @pl.when((r != holder) & (r % 2 == holder % 2))
    def _():
        copy(vc, vc, vc_send.at[0], vc_recv.at[0], mate, c).start()

    copy(kin.at[0], kin.at[0], k_send.at[0], k_recv.at[0], r, c).wait_recv()
    kpair[...] = kpart[rows(r % 2, half), :] + kin[0]
    for d in range(1, nrows // 2):
        go(copy(kpair, kin.at[d], k_send.at[d], k_recv.at[d], lax.rem(r + 2 * d, nrows), c))

    vc_two = split(vc[...])

    def first(i):
        span = pl.ds(pl.multiple_of(i * tile, tile), tile)
        out_ref[span, :] = a_ref[span, :] - mult(split(sr[span, :]), vc_two, NT)
    tile_loop(tiles, first)

    for d in range(1, nrows // 2):
        copy(kpair, kin.at[d], k_send.at[d], k_recv.at[d], r, c).wait_recv()
    summed = kpair[...]
    for d in range(1, nrows // 2):
        summed = summed + kin[d]
    mine_half = kfull.at[rows(r % 2, half)]
    mine_half[...] = summed
    go(copy(mine_half, mine_half, kg_send.at[0], kg_recv.at[0], mate, c))
    other_half = kfull.at[rows(mate % 2, half)]
    copy(other_half, other_half, kg_send.at[0], kg_recv.at[0], r, c).wait_recv()

    k_two = split(kfull[...])
    y_two = split(sc[...] - mult(vc_two, k_two))

    def second(i):
        span = pl.ds(pl.multiple_of(i * tile, tile), tile)
        out_ref[span, :] = out_ref[span, :] - mult(split(vr[span, :]), y_two, NT)
    tile_loop(tiles, second)
    corr_ref[...] = sr[rows(c, blk), :] - 0.5 * mult(split(panel_ref[...]), k_two)

    finish()


def per_device(nrows, ncols, matrix, panel, factor):
    total, wide = matrix.shape
    blk, width = panel.shape
    tile = min(256, total)
    tiles = total // tile
    group = ncols // (2 * nrows)
    lines = ncols // 2
    dma = pltpu.SemaphoreType.DMA
    vmem = pl.BlockSpec(memory_space=pltpu.VMEM)
    return pl.pallas_call(
        functools.partial(kernel, nrows, ncols, tile),
        out_shape=(jax.ShapeDtypeStruct(matrix.shape, F32), jax.ShapeDtypeStruct(panel.shape, F32)),
        in_specs=[vmem] * 3,
        out_specs=(vmem, vmem),
        scratch_shapes=[
            pltpu.VMEM((total, width), F32),
            pltpu.VMEM((wide, width), F32),
            pltpu.VMEM((total, width), F32),
            pltpu.VMEM((wide, width), F32),
            pltpu.VMEM((wide, width), F32),
            pltpu.VMEM((nrows, blk, width), F32),
            pltpu.VMEM((width, width), F32),
            pltpu.VMEM((nrows // 2, width // 2, width), F32),
            pltpu.VMEM((width // 2, width), F32),
            pltpu.VMEM((width, width), F32),
            pltpu.VMEM((tiles, wide, tile), BF16),
            pltpu.VMEM((tiles, wide, tile), BF16),
            pltpu.VMEM((tiles, width, tile), BF16),
            pltpu.VMEM((tiles, width, tile), BF16),
            dma((lines,)), dma((lines,)), dma((lines,)), dma((lines,)),
            dma((nrows,)), dma((nrows,)), dma((nrows,)), dma((nrows,)),
            dma((lines,)), dma((nrows * group,)), dma((nrows * group,)), dma((nrows * group,)),
            dma((nrows,)), dma((1,)), dma((nrows,)), dma((nrows,)), dma((nrows,)), dma((nrows,)),
        ],
        compiler_params=pltpu.CompilerParams(
            collective_id=0, has_side_effects=True, vmem_limit_bytes=60 * 1024 * 1024),
    )(matrix, panel, factor)


def solution(mesh):
    in_specs = (P("row", "col"), P(("row", "col"), None), P())
    out_specs = (P("row", "col"), P(("row", "col"), None))
    return jax.shard_map(
        functools.partial(per_device, mesh.shape["row"], mesh.shape["col"]),
        mesh=mesh, in_specs=in_specs, out_specs=out_specs, check_vma=False)
```

```python
import functools

import jax
import jax.numpy as jnp
from jax import lax
from jax.experimental import pallas as pl
from jax.experimental.pallas import tpu as pltpu
from jax.sharding import PartitionSpec as P

F32 = jnp.float32
BF16 = jnp.bfloat16
NN = (((1,), (0,)), ((), ()))
NT = (((1,), (1,)), ((), ()))


def split(x):
    high = x.astype(BF16)
    return high, (x - high.astype(F32)).astype(BF16)


def mult(a, b, dims=NN):
    dot = functools.partial(lax.dot_general, dimension_numbers=dims, preferred_element_type=F32)
    return dot(a[0], b[1]) + dot(a[1], b[0]) + dot(a[0], b[0])


def tile_loop(count, body):
    if count <= 2:
        for i in range(count):
            body(i)
    else:
        pl.loop(0, count)(body)


def kernel(nrows, ncols, tile, a_ref, panel_ref, t_ref, out_ref, corr_ref,
           vr, vc, sr, sc, q, qin, kpart, kin, kpair, kfull, at_hi, at_lo, vt_hi, vt_lo,
           v_send, v_recv, vf_send, vf_recv, q_send, q_recv, sc_send, sc_recv,
           s_send, s_recv, sf_send, sf_recv, vc_send, vc_recv, k_send, k_recv, kg_send, kg_recv):
    r, c = lax.axis_index("row"), lax.axis_index("col")
    lines = ncols // 2
    group = ncols // (2 * nrows)
    z, y = c // 2, c % 2
    blk, width = panel_ref.shape
    total = a_ref.shape[0]
    tiles = total // tile
    half = width // 2
    mate = r + 1 - 2 * (r % 2)

    def rows(index, size):
        return pl.ds(pl.multiple_of(index * size, size), size)

    def copy(src, dst, send, recv, row, col):
        return pltpu.make_async_remote_copy(
            src_ref=src, dst_ref=dst, send_sem=send, recv_sem=recv,
            device_id=(row, col), device_id_type=pl.DeviceIdType.MESH)

    barrier = pltpu.get_barrier_semaphore()

    def greet(row, col):
        pl.semaphore_signal(barrier, inc=1, device_id=(row, col), device_id_type=pl.DeviceIdType.MESH)

    target = z // group
    for d in range(1, lines):
        greet(r, lax.rem(z + d, lines) * 2 + y)
    greet(r, z * 2 + 1 - y)
    for d in range(1, nrows):
        greet(lax.rem(r + d, nrows), c)
    for g in range(group):
        line = r * group + g

        @pl.when(z != line)
        def _():
            for d in range(1, nrows):
                greet(lax.rem(r + d, nrows), line * 2 + y)

    vr[rows(c, blk), :] = panel_ref[...]
    pl.semaphore_wait(barrier, lines + nrows - 1 + jnp.where(target == r, 0, lines - 1))
    sends = []
    holder = c * nrows // ncols
    first_block = lax.rem(c * nrows, ncols)
    near = sorted((o for o in range(1 - lines, lines) if o), key=abs)

    def each_line(offsets, body):
        for o in offsets:
            line = z + o
            pl.when((line >= 0) & (line < lines))(functools.partial(body, line))

    def finish():
        for desc in sends:
            desc.wait_send()
        for d in range(lines):
            line = lax.rem(z + d, lines)
            copy(panel_ref, panel_ref, v_send.at[line], v_recv.at[line], r, c).wait_send()
            if d:
                copy(panel_ref, panel_ref, vf_send.at[line], vf_recv.at[line], r, c).wait_send()
                copy(panel_ref, panel_ref, s_send.at[line], s_recv.at[0], r, c).wait_send()

        for i in range(nrows * group):
            copy(panel_ref, panel_ref, sf_send.at[i], sf_recv.at[i], r, c).wait_send()

        @pl.when(r % 2 == holder % 2)
        def _():
            copy(vc, vc, vc_send.at[0], vc_recv.at[0], r, c).wait_send()

        @pl.when(r == holder)
        def _():
            for d in range(1, nrows // 2):
                copy(vc, vc, vc_send.at[d], vc_recv.at[0], r, c).wait_send()

    def go(desc):
        desc.start()
        sends.append(desc)

    across = z * 2 + 1 - y
    own = vr.at[rows(c, blk)]
    copy(panel_ref, own, v_send.at[z], v_recv.at[z], r, across).start()

    def send_panel(line):
        copy(panel_ref, own, v_send.at[line], v_recv.at[z], r, line * 2 + y).start()
    each_line(near, send_panel)

    def flip(i):
        lo_i = pl.ds(pl.multiple_of(i * tile, tile), tile)
        high, low = split(a_ref[lo_i, :].T)
        at_hi[i] = high
        at_lo[i] = low
    tile_loop(tiles, flip)
    t_two = split(t_ref[...])

    def forward(line):
        slot = vr.at[rows(line * 2 + y, blk)]
        copy(slot, slot, v_send.at[line], v_recv.at[line], r, c).wait_recv()
        copy(slot, slot, vf_send.at[line], vf_recv.at[line], r, across).start()

    def arrive(line):
        slot = vr.at[rows(line * 2 + 1 - y, blk)]
        copy(slot, slot, vf_send.at[line], vf_recv.at[line], r, c).wait_recv()

    each_line(near[:2], forward)
    slot = vr.at[rows(across, blk)]
    copy(slot, slot, v_send.at[z], v_recv.at[z], r, c).wait_recv()
    each_line(near[2:], forward)
    each_line(near, arrive)

    q[...] = jnp.zeros_like(q)

    def gather_product(i):
        q[...] += mult((at_hi[i], at_lo[i]), split(vr[pl.ds(pl.multiple_of(i * tile, tile), tile), :]))
    tile_loop(tiles, gather_product)

    for d in range(1, nrows):
        other = lax.rem(r + d, nrows)
        go(copy(q.at[rows(other, blk)], qin.at[d], q_send.at[d], q_recv.at[d], other, c))

    def turn(i):
        high, low = split(mult(split(vr[pl.ds(pl.multiple_of(i * tile, tile), tile), :]), t_two).T)
        vt_hi[i] = high
        vt_lo[i] = low
    tile_loop(tiles, turn)

    for d in range(1, nrows):
        copy(qin.at[d], qin.at[d], q_send.at[d], q_recv.at[d], r, c).wait_recv()
    product = q[rows(r, blk), :]
    for d in range(1, nrows):
        product = product + qin[d]
    mine = sc.at[rows(r, blk)]
    sc[rows(r, blk), :] = mult(split(product), t_two)

    local = lax.rem(c * nrows + r, ncols)
    here = r * group + lax.rem(z, group)

    def send_scaled(line):
        copy(mine, sr.at[rows(local, blk)], s_send.at[line], s_recv.at[here], target, line * 2 + y).start()
    each_line(near[::-1], send_scaled)
    for d in range(1, nrows):
        go(copy(mine, mine, sc_send.at[d], sc_recv.at[d], lax.rem(r + d, nrows), c))

    for d in range(1, nrows):
        slot = sc.at[rows(lax.rem(r - d + nrows, nrows), blk)]
        copy(slot, slot, sc_send.at[d], sc_recv.at[d], r, c).wait_recv()

    for g in range(group):
        line = r * group + g
        for d in range(nrows):
            j = lax.rem(r + d, nrows)
            place = lax.rem((line * 2 + y) * nrows + j, ncols)
            slot = sr.at[rows(place, blk)]

            @pl.when(z == line)
            def _():
                held = sc.at[rows(j, blk)]
                copy(held, slot, sf_send.at[j * group + g], sf_recv.at[j * group + g], r, across).start()
                slot[...] = held[...]

            @pl.when(z != line)
            def _():
                copy(slot, slot, s_send.at[0], s_recv.at[j * group + g], r, c).wait_recv()
                copy(slot, slot, sf_send.at[j * group + g], sf_recv.at[j * group + g], r, across).start()
    @pl.when(r == holder)
    def _():
        v_slice = vr.at[rows(first_block // nrows, nrows * blk)]
        for d in range(1, nrows // 2):
            copy(v_slice, vc, vc_send.at[d], vc_recv.at[0], lax.rem(r + 2 * d, nrows), c).start()
        copy(v_slice, vc, vc_send.at[0], vc_recv.at[0], mate, c).start()
        vc[...] = v_slice[...]

    for g in range(group):
        line = r * group + g
        for j in range(nrows):
            place = lax.rem((line * 2 + 1 - y) * nrows + j, ncols)
            slot = sr.at[rows(place, blk)]
            copy(slot, slot, sf_send.at[j * group + g], sf_recv.at[j * group + g], r, c).wait_recv()

    kpart[...] = jnp.zeros_like(kpart)

    def inner(i):
        kpart[...] += mult((vt_hi[i], vt_lo[i]), split(sr[pl.ds(pl.multiple_of(i * tile, tile), tile), :]))
    tile_loop(tiles, inner)

    go(copy(kpart.at[rows(mate % 2, half)], kin.at[0], k_send.at[0], k_recv.at[0], mate, c))

    @pl.when(r != holder)
    def _():
        copy(vc, vc, vc_send.at[0], vc_recv.at[0], r, c).wait_recv()

    @pl.when((r != holder) & (r % 2 == holder % 2))
    def _():
        copy(vc, vc, vc_send.at[0], vc_recv.at[0], mate, c).start()

    copy(kin.at[0], kin.at[0], k_send.at[0], k_recv.at[0], r, c).wait_recv()
    kpair[...] = kpart[rows(r % 2, half), :] + kin[0]
    for d in range(1, nrows // 2):
        go(copy(kpair, kin.at[d], k_send.at[d], k_recv.at[d], lax.rem(r + 2 * d, nrows), c))

    vc_two = split(vc[...])

    def first(i):
        span = pl.ds(pl.multiple_of(i * tile, tile), tile)
        out_ref[span, :] = a_ref[span, :] - mult(split(sr[span, :]), vc_two, NT)
    tile_loop(tiles, first)

    for d in range(1, nrows // 2):
        copy(kpair, kin.at[d], k_send.at[d], k_recv.at[d], r, c).wait_recv()
    summed = kpair[...]
    for d in range(1, nrows // 2):
        summed = summed + kin[d]
    mine_half = kfull.at[rows(r % 2, half)]
    mine_half[...] = summed
    go(copy(mine_half, mine_half, kg_send.at[0], kg_recv.at[0], mate, c))
    other_half = kfull.at[rows(mate % 2, half)]
    copy(other_half, other_half, kg_send.at[0], kg_recv.at[0], r, c).wait_recv()

    k_two = split(kfull[...])
    y_two = split(sc[...] - mult(vc_two, k_two))

    def second(i):
        span = pl.ds(pl.multiple_of(i * tile, tile), tile)
        out_ref[span, :] = out_ref[span, :] - mult(split(vr[span, :]), y_two, NT)
    tile_loop(tiles, second)
    corr_ref[...] = sr[rows(c, blk), :] - 0.5 * mult(split(panel_ref[...]), k_two)

    finish()


def hand_out(held_ref, held_corr_ref, out_ref, corr_ref):
    out_ref[...] = held_ref[...]
    corr_ref[...] = held_corr_ref[...]


def per_device(nrows, ncols, matrix, panel, factor):
    total, wide = matrix.shape
    blk, width = panel.shape
    tile = min(256, total)
    tiles = total // tile
    group = ncols // (2 * nrows)
    lines = ncols // 2
    dma = pltpu.SemaphoreType.DMA
    vmem = pl.BlockSpec(memory_space=pltpu.VMEM)
    limit = 4 * (5 * total * wide + 4 * total * width + 4 * wide * width + 16 * width * width) + (4 << 20)
    held = pl.pallas_call(
        functools.partial(kernel, nrows, ncols, tile),
        out_shape=(jax.ShapeDtypeStruct(matrix.shape, F32), jax.ShapeDtypeStruct(panel.shape, F32)),
        in_specs=[vmem] * 3,
        out_specs=(vmem, vmem),
        scratch_shapes=[
            pltpu.VMEM((total, width), F32),
            pltpu.VMEM((wide, width), F32),
            pltpu.VMEM((total, width), F32),
            pltpu.VMEM((wide, width), F32),
            pltpu.VMEM((wide, width), F32),
            pltpu.VMEM((nrows, blk, width), F32),
            pltpu.VMEM((width, width), F32),
            pltpu.VMEM((nrows // 2, width // 2, width), F32),
            pltpu.VMEM((width // 2, width), F32),
            pltpu.VMEM((width, width), F32),
            pltpu.VMEM((tiles, wide, tile), BF16),
            pltpu.VMEM((tiles, wide, tile), BF16),
            pltpu.VMEM((tiles, width, tile), BF16),
            pltpu.VMEM((tiles, width, tile), BF16),
            dma((lines,)), dma((lines,)), dma((lines,)), dma((lines,)),
            dma((nrows,)), dma((nrows,)), dma((nrows,)), dma((nrows,)),
            dma((lines,)), dma((nrows * group,)), dma((nrows * group,)), dma((nrows * group,)),
            dma((nrows,)), dma((1,)), dma((nrows,)), dma((nrows,)), dma((nrows,)), dma((nrows,)),
        ],
        compiler_params=pltpu.CompilerParams(
            collective_id=0, has_side_effects=True, vmem_limit_bytes=limit),
    )(matrix, panel, factor)
    return pl.pallas_call(
        hand_out,
        out_shape=(jax.ShapeDtypeStruct(matrix.shape, F32), jax.ShapeDtypeStruct(panel.shape, F32)),
        in_specs=[vmem] * 2,
        out_specs=(vmem, vmem),
        compiler_params=pltpu.CompilerParams(vmem_limit_bytes=6 * total * wide * 4 + (1 << 20)),
    )(*held)


def solution(mesh):
    in_specs = (P("row", "col"), P(("row", "col"), None), P())
    out_specs = (P("row", "col"), P(("row", "col"), None))
    return jax.shard_map(
        functools.partial(per_device, mesh.shape["row"], mesh.shape["col"]),
        mesh=mesh, in_specs=in_specs, out_specs=out_specs, check_vma=False)
```

```python
import functools

import jax
import jax.numpy as jnp
from jax import lax
from jax.experimental import pallas as pl
from jax.experimental.pallas import tpu as pltpu
from jax.sharding import PartitionSpec as P

F32 = jnp.float32
BF16 = jnp.bfloat16
NN = (((1,), (0,)), ((), ()))
NT = (((1,), (1,)), ((), ()))


def split(x):
    high = x.astype(BF16)
    return high, (x - high.astype(F32)).astype(BF16)


def mult(a, b, dims=NN):
    dot = functools.partial(lax.dot_general, dimension_numbers=dims, preferred_element_type=F32)
    return dot(a[0], b[1]) + dot(a[1], b[0]) + dot(a[0], b[0])


def tile_loop(count, body):
    if count <= 2:
        for i in range(count):
            body(i)
    else:
        pl.loop(0, count)(body)


def kernel(nrows, ncols, tile, a_ref, panel_ref, t_ref, out_ref, corr_ref,
           vr, vc, sr, sc, q, qin, kpart, kin, kpair, kfull, at_hi, at_lo, vt_hi, vt_lo,
           v_send, v_recv, vf_send, vf_recv, q_send, q_recv, sc_send, sc_recv,
           s_send, s_recv, sf_send, sf_recv, vc_send, vc_recv, k_send, k_recv, kg_send, kg_recv):
    r, c = lax.axis_index("row"), lax.axis_index("col")
    lines = ncols // 2
    group = ncols // (2 * nrows)
    z, y = c // 2, c % 2
    blk, width = panel_ref.shape
    total = a_ref.shape[0]
    tiles = total // tile
    half = width // 2
    mate = r + 1 - 2 * (r % 2)

    def rows(index, size):
        return pl.ds(pl.multiple_of(index * size, size), size)

    def copy(src, dst, send, recv, row, col):
        return pltpu.make_async_remote_copy(
            src_ref=src, dst_ref=dst, send_sem=send, recv_sem=recv,
            device_id=(row, col), device_id_type=pl.DeviceIdType.MESH)

    barrier = pltpu.get_barrier_semaphore()

    def greet(row, col):
        pl.semaphore_signal(barrier, inc=1, device_id=(row, col), device_id_type=pl.DeviceIdType.MESH)

    target = z // group
    for d in range(1, lines):
        greet(r, lax.rem(z + d, lines) * 2 + y)
    greet(r, z * 2 + 1 - y)
    for d in range(1, nrows):
        greet(lax.rem(r + d, nrows), c)
    for g in range(group):
        line = r * group + g

        @pl.when(z != line)
        def _():
            for d in range(1, nrows):
                greet(lax.rem(r + d, nrows), line * 2 + y)

    vr[rows(c, blk), :] = panel_ref[...]
    pl.semaphore_wait(barrier, lines + nrows - 1 + jnp.where(target == r, 0, lines - 1))
    sends = []
    holder = c * nrows // ncols
    first_block = lax.rem(c * nrows, ncols)

    def each_line(body, sign):
        for d in range(1, lines):
            body(lax.rem(z + sign * d + lines, lines))

    def finish():
        for desc in sends:
            desc.wait_send()
        for d in range(lines):
            line = lax.rem(z + d, lines)
            copy(panel_ref, panel_ref, v_send.at[line], v_recv.at[line], r, c).wait_send()
            if d:
                copy(panel_ref, panel_ref, vf_send.at[line], vf_recv.at[line], r, c).wait_send()
                copy(panel_ref, panel_ref, s_send.at[line], s_recv.at[0], r, c).wait_send()

        for i in range(nrows * group):
            copy(panel_ref, panel_ref, sf_send.at[i], sf_recv.at[i], r, c).wait_send()

        @pl.when(r % 2 == holder % 2)
        def _():
            copy(vc, vc, vc_send.at[0], vc_recv.at[0], r, c).wait_send()

        @pl.when(r == holder)
        def _():
            for d in range(1, nrows // 2):
                copy(vc, vc, vc_send.at[d], vc_recv.at[0], r, c).wait_send()

    def go(desc):
        desc.start()
        sends.append(desc)

    across = z * 2 + 1 - y
    own = vr.at[rows(c, blk)]
    copy(panel_ref, own, v_send.at[z], v_recv.at[z], r, across).start()

    def send_panel(line):
        copy(panel_ref, own, v_send.at[line], v_recv.at[z], r, line * 2 + y).start()
    each_line(send_panel, 1)

    def flip(i):
        lo_i = pl.ds(pl.multiple_of(i * tile, tile), tile)
        high, low = split(a_ref[lo_i, :].T)
        at_hi[i] = high
        at_lo[i] = low
    tile_loop(tiles, flip)
    t_two = split(t_ref[...])

    def forward(line):
        slot = vr.at[rows(line * 2 + y, blk)]
        copy(slot, slot, v_send.at[line], v_recv.at[line], r, c).wait_recv()
        copy(slot, slot, vf_send.at[line], vf_recv.at[line], r, across).start()

    def arrive(line):
        slot = vr.at[rows(line * 2 + 1 - y, blk)]
        copy(slot, slot, vf_send.at[line], vf_recv.at[line], r, c).wait_recv()

    each_line(forward, -1)
    slot = vr.at[rows(across, blk)]
    copy(slot, slot, v_send.at[z], v_recv.at[z], r, c).wait_recv()
    each_line(arrive, -1)

    q[...] = jnp.zeros_like(q)

    def gather_product(i):
        q[...] += mult((at_hi[i], at_lo[i]), split(vr[pl.ds(pl.multiple_of(i * tile, tile), tile), :]))
    tile_loop(tiles, gather_product)

    for d in range(1, nrows):
        other = lax.rem(r + d, nrows)
        go(copy(q.at[rows(other, blk)], qin.at[d], q_send.at[d], q_recv.at[d], other, c))

    def turn(i):
        high, low = split(mult(split(vr[pl.ds(pl.multiple_of(i * tile, tile), tile), :]), t_two).T)
        vt_hi[i] = high
        vt_lo[i] = low
    tile_loop(tiles, turn)

    for d in range(1, nrows):
        copy(qin.at[d], qin.at[d], q_send.at[d], q_recv.at[d], r, c).wait_recv()
    product = q[rows(r, blk), :]
    for d in range(1, nrows):
        product = product + qin[d]
    mine = sc.at[rows(r, blk)]
    sc[rows(r, blk), :] = mult(split(product), t_two)

    local = lax.rem(c * nrows + r, ncols)
    here = r * group + lax.rem(z, group)

    def send_scaled(line):
        copy(mine, sr.at[rows(local, blk)], s_send.at[line], s_recv.at[here], target, line * 2 + y).start()
    each_line(send_scaled, 1)
    for d in range(1, nrows):
        go(copy(mine, mine, sc_send.at[d], sc_recv.at[d], lax.rem(r + d, nrows), c))

    for d in range(1, nrows):
        slot = sc.at[rows(lax.rem(r - d + nrows, nrows), blk)]
        copy(slot, slot, sc_send.at[d], sc_recv.at[d], r, c).wait_recv()

    for g in range(group):
        line = r * group + g
        for d in range(nrows):
            j = lax.rem(r + d, nrows)
            place = lax.rem((line * 2 + y) * nrows + j, ncols)
            slot = sr.at[rows(place, blk)]

            @pl.when(z == line)
            def _():
                held = sc.at[rows(j, blk)]
                copy(held, slot, sf_send.at[j * group + g], sf_recv.at[j * group + g], r, across).start()
                slot[...] = held[...]

            @pl.when(z != line)
            def _():
                copy(slot, slot, s_send.at[0], s_recv.at[j * group + g], r, c).wait_recv()
                copy(slot, slot, sf_send.at[j * group + g], sf_recv.at[j * group + g], r, across).start()
    @pl.when(r == holder)
    def _():
        v_slice = vr.at[rows(first_block // nrows, nrows * blk)]
        for d in range(1, nrows // 2):
            copy(v_slice, vc, vc_send.at[d], vc_recv.at[0], lax.rem(r + 2 * d, nrows), c).start()
        copy(v_slice, vc, vc_send.at[0], vc_recv.at[0], mate, c).start()
        vc[...] = v_slice[...]

    for g in range(group):
        line = r * group + g
        for j in range(nrows):
            place = lax.rem((line * 2 + 1 - y) * nrows + j, ncols)
            slot = sr.at[rows(place, blk)]
            copy(slot, slot, sf_send.at[j * group + g], sf_recv.at[j * group + g], r, c).wait_recv()

    kpart[...] = jnp.zeros_like(kpart)

    def inner(i):
        kpart[...] += mult((vt_hi[i], vt_lo[i]), split(sr[pl.ds(pl.multiple_of(i * tile, tile), tile), :]))
    tile_loop(tiles, inner)

    go(copy(kpart.at[rows(mate % 2, half)], kin.at[0], k_send.at[0], k_recv.at[0], mate, c))

    @pl.when(r != holder)
    def _():
        copy(vc, vc, vc_send.at[0], vc_recv.at[0], r, c).wait_recv()

    @pl.when((r != holder) & (r % 2 == holder % 2))
    def _():
        copy(vc, vc, vc_send.at[0], vc_recv.at[0], mate, c).start()

    copy(kin.at[0], kin.at[0], k_send.at[0], k_recv.at[0], r, c).wait_recv()
    kpair[...] = kpart[rows(r % 2, half), :] + kin[0]
    for d in range(1, nrows // 2):
        go(copy(kpair, kin.at[d], k_send.at[d], k_recv.at[d], lax.rem(r + 2 * d, nrows), c))

    vc_two = split(vc[...])

    def first(i):
        span = pl.ds(pl.multiple_of(i * tile, tile), tile)
        out_ref[span, :] = a_ref[span, :] - mult(split(sr[span, :]), vc_two, NT)
    tile_loop(tiles, first)

    for d in range(1, nrows // 2):
        copy(kpair, kin.at[d], k_send.at[d], k_recv.at[d], r, c).wait_recv()
    summed = kpair[...]
    for d in range(1, nrows // 2):
        summed = summed + kin[d]
    mine_half = kfull.at[rows(r % 2, half)]
    mine_half[...] = summed
    go(copy(mine_half, mine_half, kg_send.at[0], kg_recv.at[0], mate, c))
    other_half = kfull.at[rows(mate % 2, half)]
    copy(other_half, other_half, kg_send.at[0], kg_recv.at[0], r, c).wait_recv()

    k_two = split(kfull[...])
    y_two = split(sc[...] - mult(vc_two, k_two))

    def second(i):
        span = pl.ds(pl.multiple_of(i * tile, tile), tile)
        out_ref[span, :] = out_ref[span, :] - mult(split(vr[span, :]), y_two, NT)
    tile_loop(tiles, second)
    corr_ref[...] = sr[rows(c, blk), :] - 0.5 * mult(split(panel_ref[...]), k_two)

    finish()


def hand_out(held_ref, held_corr_ref, out_ref, corr_ref):
    out_ref[...] = held_ref[...]
    corr_ref[...] = held_corr_ref[...]


def per_device(nrows, ncols, matrix, panel, factor):
    total, wide = matrix.shape
    blk, width = panel.shape
    tile = min(256, total)
    tiles = total // tile
    group = ncols // (2 * nrows)
    lines = ncols // 2
    dma = pltpu.SemaphoreType.DMA
    vmem = pl.BlockSpec(memory_space=pltpu.VMEM)
    limit = 4 * (5 * total * wide + 4 * total * width + 4 * wide * width + 16 * width * width) + (4 << 20)
    held = pl.pallas_call(
        functools.partial(kernel, nrows, ncols, tile),
        out_shape=(jax.ShapeDtypeStruct(matrix.shape, F32), jax.ShapeDtypeStruct(panel.shape, F32)),
        in_specs=[vmem] * 3,
        out_specs=(vmem, vmem),
        scratch_shapes=[
            pltpu.VMEM((total, width), F32),
            pltpu.VMEM((wide, width), F32),
            pltpu.VMEM((total, width), F32),
            pltpu.VMEM((wide, width), F32),
            pltpu.VMEM((wide, width), F32),
            pltpu.VMEM((nrows, blk, width), F32),
            pltpu.VMEM((width, width), F32),
            pltpu.VMEM((nrows // 2, width // 2, width), F32),
            pltpu.VMEM((width // 2, width), F32),
            pltpu.VMEM((width, width), F32),
            pltpu.VMEM((tiles, wide, tile), BF16),
            pltpu.VMEM((tiles, wide, tile), BF16),
            pltpu.VMEM((tiles, width, tile), BF16),
            pltpu.VMEM((tiles, width, tile), BF16),
            dma((lines,)), dma((lines,)), dma((lines,)), dma((lines,)),
            dma((nrows,)), dma((nrows,)), dma((nrows,)), dma((nrows,)),
            dma((lines,)), dma((nrows * group,)), dma((nrows * group,)), dma((nrows * group,)),
            dma((nrows,)), dma((1,)), dma((nrows,)), dma((nrows,)), dma((nrows,)), dma((nrows,)),
        ],
        compiler_params=pltpu.CompilerParams(
            collective_id=0, has_side_effects=True, vmem_limit_bytes=limit),
    )(matrix, panel, factor)
    return pl.pallas_call(
        hand_out,
        out_shape=(jax.ShapeDtypeStruct(matrix.shape, F32), jax.ShapeDtypeStruct(panel.shape, F32)),
        in_specs=[vmem] * 2,
        out_specs=(vmem, vmem),
        compiler_params=pltpu.CompilerParams(vmem_limit_bytes=6 * total * wide * 4 + (1 << 20)),
    )(*held)


def solution(mesh):
    in_specs = (P("row", "col"), P(("row", "col"), None), P())
    out_specs = (P("row", "col"), P(("row", "col"), None))
    return jax.shard_map(
        functools.partial(per_device, mesh.shape["row"], mesh.shape["col"]),
        mesh=mesh, in_specs=in_specs, out_specs=out_specs, check_vma=False)
```

```python
import functools

import jax
import jax.numpy as jnp
from jax import lax
from jax.experimental import pallas as pl
from jax.experimental.pallas import tpu as pltpu
from jax.sharding import PartitionSpec as P

F32 = jnp.float32
BF16 = jnp.bfloat16
NN = (((1,), (0,)), ((), ()))
NT = (((1,), (1,)), ((), ()))


def split(x):
    high = x.astype(BF16)
    return high, (x - high.astype(F32)).astype(BF16)


def mult(a, b, dims=NN):
    dot = functools.partial(lax.dot_general, dimension_numbers=dims, preferred_element_type=F32)
    return dot(a[0], b[1]) + dot(a[1], b[0]) + dot(a[0], b[0])


def tile_loop(count, body):
    if count <= 2:
        for i in range(count):
            body(i)
    else:
        pl.loop(0, count)(body)


def kernel(nrows, ncols, tile, a_ref, panel_ref, t_ref, out_ref, corr_ref,
           vr, vc, sr, sc, q, qin, kpart, kin, kpair, kfull, at_hi, at_lo, vt_hi, vt_lo,
           v_send, v_recv, vf_send, vf_recv, q_send, q_recv, sc_send, sc_recv,
           s_send, s_recv, sf_send, sf_recv, vc_send, vc_recv, k_send, k_recv, kg_send, kg_recv):
    r, c = lax.axis_index("row"), lax.axis_index("col")
    lines = ncols // 2
    group = ncols // (2 * nrows)
    z, y = c // 2, c % 2
    blk, width = panel_ref.shape
    total = a_ref.shape[0]
    tiles = total // tile
    half = width // 2
    mate = r + 1 - 2 * (r % 2)

    def rows(index, size):
        return pl.ds(pl.multiple_of(index * size, size), size)

    def copy(src, dst, send, recv, row, col):
        return pltpu.make_async_remote_copy(
            src_ref=src, dst_ref=dst, send_sem=send, recv_sem=recv,
            device_id=(row, col), device_id_type=pl.DeviceIdType.MESH)

    barrier = pltpu.get_barrier_semaphore()

    def greet(row, col):
        pl.semaphore_signal(barrier, inc=1, device_id=(row, col), device_id_type=pl.DeviceIdType.MESH)

    target = z // group
    for d in range(1, lines):
        greet(r, lax.rem(z + d, lines) * 2 + y)
    greet(r, z * 2 + 1 - y)
    opposite = lax.rem(z + lines // 2, lines)
    greet(r, opposite * 2 + 1 - y)
    for d in range(1, nrows):
        greet(lax.rem(r + d, nrows), c)
    for g in range(group):
        line = r * group + g

        @pl.when(z != line)
        def _():
            for d in range(1, nrows):
                greet(lax.rem(r + d, nrows), line * 2 + y)

    vr[rows(c, blk), :] = panel_ref[...]
    pl.semaphore_wait(barrier, lines + nrows + jnp.where(target == r, 0, lines - 1))
    sends = []
    holder = c * nrows // ncols
    first_block = lax.rem(c * nrows, ncols)

    def each_line(body, sign, skip=0):
        for d in range(1, lines):
            if d == skip:
                continue
            body(lax.rem(z + sign * d + lines, lines))

    def finish():
        for desc in sends:
            desc.wait_send()
        for d in range(lines):
            line = lax.rem(z + d, lines)
            copy(panel_ref, panel_ref, v_send.at[line], v_recv.at[line], r, c).wait_send()
            if d:
                copy(panel_ref, panel_ref, vf_send.at[line], vf_recv.at[line], r, c).wait_send()
                copy(panel_ref, panel_ref, s_send.at[line], s_recv.at[0], r, c).wait_send()

        for i in range(nrows * group):
            copy(panel_ref, panel_ref, sf_send.at[i], sf_recv.at[i], r, c).wait_send()

        @pl.when(r % 2 == holder % 2)
        def _():
            copy(vc, vc, vc_send.at[0], vc_recv.at[0], r, c).wait_send()

        @pl.when(r == holder)
        def _():
            for d in range(1, nrows // 2):
                copy(vc, vc, vc_send.at[d], vc_recv.at[0], r, c).wait_send()

    def go(desc):
        desc.start()
        sends.append(desc)

    across = z * 2 + 1 - y
    own = vr.at[rows(c, blk)]
    copy(panel_ref, own, v_send.at[z], v_recv.at[z], r, across).start()

    def send_panel(line):
        copy(panel_ref, own, v_send.at[line], v_recv.at[z], r, line * 2 + y).start()
    each_line(send_panel, 1)
    copy(panel_ref, own, vf_send.at[opposite], vf_recv.at[z], r, opposite * 2 + 1 - y).start()

    def flip(i):
        lo_i = pl.ds(pl.multiple_of(i * tile, tile), tile)
        high, low = split(a_ref[lo_i, :].T)
        at_hi[i] = high
        at_lo[i] = low
    tile_loop(tiles, flip)
    t_two = split(t_ref[...])

    def forward(line):
        slot = vr.at[rows(line * 2 + y, blk)]
        copy(slot, slot, v_send.at[line], v_recv.at[line], r, c).wait_recv()
        copy(slot, slot, vf_send.at[line], vf_recv.at[line], r, across).start()

    def arrive(line):
        slot = vr.at[rows(line * 2 + 1 - y, blk)]
        copy(slot, slot, vf_send.at[line], vf_recv.at[line], r, c).wait_recv()

    each_line(forward, -1, lines // 2)
    slot = vr.at[rows(opposite * 2 + y, blk)]
    copy(slot, slot, v_send.at[opposite], v_recv.at[opposite], r, c).wait_recv()
    slot = vr.at[rows(across, blk)]
    copy(slot, slot, v_send.at[z], v_recv.at[z], r, c).wait_recv()
    each_line(arrive, -1)

    q[...] = jnp.zeros_like(q)

    def gather_product(i):
        q[...] += mult((at_hi[i], at_lo[i]), split(vr[pl.ds(pl.multiple_of(i * tile, tile), tile), :]))
    tile_loop(tiles, gather_product)

    for d in range(1, nrows):
        other = lax.rem(r + d, nrows)
        go(copy(q.at[rows(other, blk)], qin.at[d], q_send.at[d], q_recv.at[d], other, c))

    def turn(i):
        high, low = split(mult(split(vr[pl.ds(pl.multiple_of(i * tile, tile), tile), :]), t_two).T)
        vt_hi[i] = high
        vt_lo[i] = low
    tile_loop(tiles, turn)

    for d in range(1, nrows):
        copy(qin.at[d], qin.at[d], q_send.at[d], q_recv.at[d], r, c).wait_recv()
    product = q[rows(r, blk), :]
    for d in range(1, nrows):
        product = product + qin[d]
    mine = sc.at[rows(r, blk)]
    sc[rows(r, blk), :] = mult(split(product), t_two)

    local = lax.rem(c * nrows + r, ncols)
    here = r * group + lax.rem(z, group)

    def send_scaled(line):
        copy(mine, sr.at[rows(local, blk)], s_send.at[line], s_recv.at[here], target, line * 2 + y).start()
    each_line(send_scaled, 1)
    for d in range(1, nrows):
        go(copy(mine, mine, sc_send.at[d], sc_recv.at[d], lax.rem(r + d, nrows), c))

    for d in range(1, nrows):
        slot = sc.at[rows(lax.rem(r - d + nrows, nrows), blk)]
        copy(slot, slot, sc_send.at[d], sc_recv.at[d], r, c).wait_recv()

    for g in range(group):
        line = r * group + g
        for d in range(nrows):
            j = lax.rem(r + d, nrows)
            place = lax.rem((line * 2 + y) * nrows + j, ncols)
            slot = sr.at[rows(place, blk)]

            @pl.when(z == line)
            def _():
                held = sc.at[rows(j, blk)]
                copy(held, slot, sf_send.at[j * group + g], sf_recv.at[j * group + g], r, across).start()
                slot[...] = held[...]

            @pl.when(z != line)
            def _():
                copy(slot, slot, s_send.at[0], s_recv.at[j * group + g], r, c).wait_recv()
                copy(slot, slot, sf_send.at[j * group + g], sf_recv.at[j * group + g], r, across).start()
    @pl.when(r == holder)
    def _():
        v_slice = vr.at[rows(first_block // nrows, nrows * blk)]
        for d in range(1, nrows // 2):
            copy(v_slice, vc, vc_send.at[d], vc_recv.at[0], lax.rem(r + 2 * d, nrows), c).start()
        copy(v_slice, vc, vc_send.at[0], vc_recv.at[0], mate, c).start()
        vc[...] = v_slice[...]

    for g in range(group):
        line = r * group + g
        for j in range(nrows):
            place = lax.rem((line * 2 + 1 - y) * nrows + j, ncols)
            slot = sr.at[rows(place, blk)]
            copy(slot, slot, sf_send.at[j * group + g], sf_recv.at[j * group + g], r, c).wait_recv()

    kpart[...] = jnp.zeros_like(kpart)

    def inner(i):
        kpart[...] += mult((vt_hi[i], vt_lo[i]), split(sr[pl.ds(pl.multiple_of(i * tile, tile), tile), :]))
    tile_loop(tiles, inner)

    go(copy(kpart.at[rows(mate % 2, half)], kin.at[0], k_send.at[0], k_recv.at[0], mate, c))

    @pl.when(r != holder)
    def _():
        copy(vc, vc, vc_send.at[0], vc_recv.at[0], r, c).wait_recv()

    @pl.when((r != holder) & (r % 2 == holder % 2))
    def _():
        copy(vc, vc, vc_send.at[0], vc_recv.at[0], mate, c).start()

    copy(kin.at[0], kin.at[0], k_send.at[0], k_recv.at[0], r, c).wait_recv()
    kpair[...] = kpart[rows(r % 2, half), :] + kin[0]
    for d in range(1, nrows // 2):
        go(copy(kpair, kin.at[d], k_send.at[d], k_recv.at[d], lax.rem(r + 2 * d, nrows), c))

    vc_two = split(vc[...])

    def first(i):
        span = pl.ds(pl.multiple_of(i * tile, tile), tile)
        out_ref[span, :] = a_ref[span, :] - mult(split(sr[span, :]), vc_two, NT)
    tile_loop(tiles, first)

    for d in range(1, nrows // 2):
        copy(kpair, kin.at[d], k_send.at[d], k_recv.at[d], r, c).wait_recv()
    summed = kpair[...]
    for d in range(1, nrows // 2):
        summed = summed + kin[d]
    mine_half = kfull.at[rows(r % 2, half)]
    mine_half[...] = summed
    go(copy(mine_half, mine_half, kg_send.at[0], kg_recv.at[0], mate, c))
    other_half = kfull.at[rows(mate % 2, half)]
    copy(other_half, other_half, kg_send.at[0], kg_recv.at[0], r, c).wait_recv()

    k_two = split(kfull[...])
    y_two = split(sc[...] - mult(vc_two, k_two))

    def second(i):
        span = pl.ds(pl.multiple_of(i * tile, tile), tile)
        out_ref[span, :] = out_ref[span, :] - mult(split(vr[span, :]), y_two, NT)
    tile_loop(tiles, second)
    corr_ref[...] = sr[rows(c, blk), :] - 0.5 * mult(split(panel_ref[...]), k_two)

    finish()


def hand_out(held_ref, held_corr_ref, out_ref, corr_ref):
    out_ref[...] = held_ref[...]
    corr_ref[...] = held_corr_ref[...]


def per_device(nrows, ncols, matrix, panel, factor):
    total, wide = matrix.shape
    blk, width = panel.shape
    tile = min(256, total)
    tiles = total // tile
    group = ncols // (2 * nrows)
    lines = ncols // 2
    dma = pltpu.SemaphoreType.DMA
    vmem = pl.BlockSpec(memory_space=pltpu.VMEM)
    limit = 4 * (5 * total * wide + 4 * total * width + 4 * wide * width + 16 * width * width) + (4 << 20)
    held = pl.pallas_call(
        functools.partial(kernel, nrows, ncols, tile),
        out_shape=(jax.ShapeDtypeStruct(matrix.shape, F32), jax.ShapeDtypeStruct(panel.shape, F32)),
        in_specs=[vmem] * 3,
        out_specs=(vmem, vmem),
        scratch_shapes=[
            pltpu.VMEM((total, width), F32),
            pltpu.VMEM((wide, width), F32),
            pltpu.VMEM((total, width), F32),
            pltpu.VMEM((wide, width), F32),
            pltpu.VMEM((wide, width), F32),
            pltpu.VMEM((nrows, blk, width), F32),
            pltpu.VMEM((width, width), F32),
            pltpu.VMEM((nrows // 2, width // 2, width), F32),
            pltpu.VMEM((width // 2, width), F32),
            pltpu.VMEM((width, width), F32),
            pltpu.VMEM((tiles, wide, tile), BF16),
            pltpu.VMEM((tiles, wide, tile), BF16),
            pltpu.VMEM((tiles, width, tile), BF16),
            pltpu.VMEM((tiles, width, tile), BF16),
            dma((lines,)), dma((lines,)), dma((lines,)), dma((lines,)),
            dma((nrows,)), dma((nrows,)), dma((nrows,)), dma((nrows,)),
            dma((lines,)), dma((nrows * group,)), dma((nrows * group,)), dma((nrows * group,)),
            dma((nrows,)), dma((1,)), dma((nrows,)), dma((nrows,)), dma((nrows,)), dma((nrows,)),
        ],
        compiler_params=pltpu.CompilerParams(
            collective_id=0, has_side_effects=True, vmem_limit_bytes=limit),
    )(matrix, panel, factor)
    return pl.pallas_call(
        hand_out,
        out_shape=(jax.ShapeDtypeStruct(matrix.shape, F32), jax.ShapeDtypeStruct(panel.shape, F32)),
        in_specs=[vmem] * 2,
        out_specs=(vmem, vmem),
        compiler_params=pltpu.CompilerParams(vmem_limit_bytes=6 * total * wide * 4 + (1 << 20)),
    )(*held)


def solution(mesh):
    in_specs = (P("row", "col"), P(("row", "col"), None), P())
    out_specs = (P("row", "col"), P(("row", "col"), None))
    return jax.shard_map(
        functools.partial(per_device, mesh.shape["row"], mesh.shape["col"]),
        mesh=mesh, in_specs=in_specs, out_specs=out_specs, check_vma=False)
```
